32 devices in a mesh: dp: 4 (over x, core), row: 2 (over y), col: 4 (over z).
Axes of the slice: x: 2, y: 2, z: 4, core: 2. Of those that a mesh axis runs over, the one named last changes fastest.
Arguments:
- layer_input: bfloat16 [8192, 2048], P(('dp', 'col'), 'row'), may hold values from -6 to 6
- norm_gain: float32 [2048], P('row'), may hold values from 0.3 to 2.4
- norm_shift: float32 [2048], P('row'), may hold values from -4 to 4
- qkv_weight: bfloat16 [2048, 3, 2048], P('row', None, 'col'), may hold values from -0.125 to 0.125
- qkv_bias: float32 [3, 2048], P(None, 'col'), may hold values from -16 to 16
- up_weight: bfloat16 [2048, 8192], P('row', 'col'), may hold values from -2 to 2
- up_bias: float32 [8192], P('col'), may hold values from -6 to 6
- out_weight: bfloat16 [2048, 2048], P('col', 'row'), may hold values from -0.5 to 0.5
- out_bias: float32 [2048], P('row'), may hold values from -4 to 4
- down_weight: bfloat16 [8192, 2048], P('col', 'row'), may hold values from -0.0625 to 0.0625
- down_bias: float32 [2048], P('row'), may hold values from -4 to 4
- grad_output: bfloat16 [8192, 2048], P(('dp', 'col'), 'row'), may hold values from -6 to 6
Outputs:
- layer_output: bfloat16 [8192, 2048], P(('dp', 'col'), 'row')
- grad_input: float32 [8192, 2048], P(('dp', 'col'), 'row')
- grad_gain: float32 [2048], P('row')
- grad_shift: float32 [2048], P('row')
- grad_qkv_weight: float32 [2048, 3, 2048], P('row', None, 'col')
- grad_qkv_bias: float32 [3, 2048], P(None, 'col')
- grad_up_weight: float32 [2048, 8192], P('row', 'col')
- grad_up_bias: float32 [8192], P('col')
- grad_out_weight: float32 [2048, 2048], P('col', 'row')
- grad_out_bias: float32 [2048], P('row')
- grad_down_weight: float32 [8192, 2048], P('col', 'row')
- grad_down_bias: float32 [2048], P('row')
The draws below stay inside these ranges and needn't reach their ends.
All inputs are finite; a program needn't handle non-finite values.
Results may differ from the reference program's by a relative error of at most 0.033.
The reference program's roundings to bfloat16 on the way count: a program that leaves them out, or rounds other values in their place, can miss the bound.
Values may be sent and summed in bfloat16 or wider, within the bound.
No kernel may reach another device: no remote copies, remote signals or barrier semaphores. Data moves between devices by JAX's collectives and lax.ppermute only.
A program may use at most 320 MiB of HBM per device.

```python
import math
import jax
import jax.numpy as jnp
from jax import lax

D = 2048
HEADS = 32
FF = 8192
HEAD = 64
ROT = 32
SEQ_LEN = 1024
TOKENS = 8192


def draw_qkv_bias(key, part):
    base = 0.5 * jax.random.normal(jax.random.fold_in(key, 11), (3, D), jnp.float32)
    base = jnp.clip(base, -3.0, 3.0)
    return base


def draw_norm_gain(key, part):
    place = jnp.arange(D).astype(jnp.float32) / (D - 1)
    rough = jax.random.uniform(jax.random.fold_in(key, 21), (D,), jnp.float32, -1.0, 1.0)
    trend = 0.5 * jnp.exp(math.log(3.0) * place)
    return trend * (1.0 + 0.15 * rough)


def draw_up_weight(key, part):
    scale = 1.0 / math.sqrt(D)
    main = jnp.clip(jax.random.normal(jax.random.fold_in(key, 31), (D, FF), jnp.float32), -6.0, 6.0)
    shared = jnp.clip(jax.random.normal(jax.random.fold_in(key, 32), (FF,), jnp.float32), -6.0, 6.0)
    return ((main + shared[None, :]) * scale).astype(jnp.bfloat16)


def shard_levels(stream_key, extent, split, least, top_value):
    level = 1.0
    for axis_at, blocks in split:
        heights = jax.random.uniform(jax.random.fold_in(jax.random.fold_in(stream_key, 6), axis_at), (blocks,), jnp.float32, least / len(split), top_value / len(split))
        level = level * jnp.repeat(jnp.exp(heights), extent[axis_at] // blocks).reshape((-1,) + (1,) * (len(extent) - 1 - axis_at))
    return level


def normal_values(key, extent, scale, limit, split=(), dtype=jnp.bfloat16):
    array = scale * jax.random.normal(key, extent, jnp.float32)
    if split:
        array = array * shard_levels(key, extent, split, -0.22, 0.18)
    return jnp.clip(array, -limit, limit).astype(dtype)


def setup_inputs(seed: int = 0) -> dict:
    arg_keys = jax.random.split(jax.random.key(seed), 13)
    layer_input = normal_values(arg_keys[0], (TOKENS, D), 1.0, 6.0, ((0, 16), (1, 2)))
    norm_gain = draw_norm_gain(jax.random.fold_in(arg_keys[12], 71), 0)
    norm_shift = normal_values(arg_keys[2], (D,), 0.3, 4.0, ((0, 2),), jnp.float32)
    qkv_weight = normal_values(arg_keys[3], (D, 3, D), D ** -0.5, 0.125, ((0, 2), (2, 4)))
    qkv_bias = draw_qkv_bias(jax.random.fold_in(arg_keys[12], 71), 0)
    up_weight = draw_up_weight(jax.random.fold_in(arg_keys[12], 71), 0)
    up_bias = normal_values(arg_keys[6], (FF,), 0.5, 6.0, ((0, 4),), jnp.float32)
    out_weight = normal_values(arg_keys[7], (D, D), (D // 16) ** -0.5, 0.5, ((0, 4), (1, 2)))
    out_bias = normal_values(arg_keys[8], (D,), 0.3, 4.0, ((0, 2),), jnp.float32)
    down_weight = normal_values(arg_keys[9], (FF, D), FF ** -0.5, 0.0625, ((0, 4), (1, 2)))
    down_bias = normal_values(arg_keys[10], (D,), 0.3, 4.0, ((0, 2),), jnp.float32)
    grad_output = normal_values(arg_keys[11], (TOKENS, D), 1.0, 6.0, ((0, 16), (1, 2)))
    return dict(layer_input=layer_input, norm_gain=norm_gain, norm_shift=norm_shift, qkv_weight=qkv_weight, qkv_bias=qkv_bias, up_weight=up_weight, up_bias=up_bias, out_weight=out_weight, out_bias=out_bias, down_weight=down_weight, down_bias=down_bias, grad_output=grad_output)


eps_norm = 1e-05
gelu_scale = 0.7978845608028654
gelu_cubic = 0.044715

def gelu_tanh(value):
    inner = gelu_scale * (value + gelu_cubic * value * value * value)
    return 0.5 * value * (1.0 + jnp.tanh(inner))

def gelu_slope(value):
    inner = gelu_scale * (value + gelu_cubic * value * value * value)
    tanh_val = jnp.tanh(inner)
    return 0.5 * (1.0 + tanh_val) + 0.5 * value * (1.0 - tanh_val * tanh_val) * gelu_scale * (1.0 + 3.0 * gelu_cubic * value * value)

def rotary_tables(length):
    positions = jnp.arange(length).astype(jnp.float32)
    frequency = jnp.exp(-math.log(10000.0) * jnp.arange(0, ROT, 2).astype(jnp.float32) / ROT)
    angles = positions[:, None] * frequency[None, :]
    cosine = jnp.concatenate([jnp.cos(angles), jnp.cos(angles)], axis=1)[:, None, :]
    sine_table = jnp.concatenate([jnp.sin(angles), jnp.sin(angles)], axis=1)[:, None, :]
    return (cosine, sine_table)

def rotate(field, cosine, sine_table):
    half = ROT // 2
    part = field[..., :ROT]
    turned = jnp.concatenate([-part[..., half:], part[..., :half]], axis=-1)
    return jnp.concatenate([part * cosine + turned * sine_table, field[..., ROT:]], axis=-1)

def unrotate(grad, cosine, sine_table):
    half = ROT // 2
    part = grad[..., :ROT]
    scaled = part * sine_table
    turned = jnp.concatenate([scaled[..., half:], -scaled[..., :half]], axis=-1)
    return jnp.concatenate([part * cosine + turned, grad[..., ROT:]], axis=-1)

def causal_scores(query, keys):
    scale = 1.0 / math.sqrt(HEAD)
    raw = jnp.einsum('qhd,khd->hqk', query.astype(jnp.float32), keys.astype(jnp.float32)) * scale
    rows = lax.broadcasted_iota(jnp.int32, (query.shape[0], keys.shape[0]), 0)
    cols = lax.broadcasted_iota(jnp.int32, (query.shape[0], keys.shape[0]), 1)
    return jnp.where(cols <= rows, raw, -1e+30)

def attend(query, keys, values):
    scores = causal_scores(query, keys)
    peak = lax.optimization_barrier(jnp.max(scores, axis=-1))
    total = lax.optimization_barrier(jnp.sum(jnp.exp(scores - peak[..., None]), axis=-1))
    log_total = peak + jnp.log(total)
    weights = jnp.exp(scores - log_total[..., None]).astype(jnp.bfloat16)
    output = jnp.einsum('hqk,khd->qhd', weights.astype(jnp.float32), values.astype(jnp.float32)).astype(jnp.bfloat16)
    return (output, log_total)

def attend_back(query, keys, values, output, grad_out, log_total):
    scale = 1.0 / math.sqrt(HEAD)
    scores = causal_scores(query, keys)
    probs = jnp.exp(scores - log_total[..., None])
    weights = probs.astype(jnp.bfloat16).astype(jnp.float32)
    grad_float = grad_out.astype(jnp.float32)
    along = jnp.einsum('qhd,khd->hqk', grad_float, values.astype(jnp.float32))
    delta = lax.optimization_barrier(jnp.sum(grad_float * output.astype(jnp.float32), axis=-1)).T
    grad_scores = (probs * (along - delta[..., None])).astype(jnp.bfloat16).astype(jnp.float32)
    grad_values = jnp.einsum('hqk,qhd->khd', weights, grad_float)
    grad_query = jnp.einsum('hqk,khd->qhd', grad_scores, keys.astype(jnp.float32)) * scale
    grad_keys = jnp.einsum('hqk,qhd->khd', grad_scores, query.astype(jnp.float32)) * scale
    return (grad_query, grad_keys, grad_values)

def reference(layer_input, norm_gain, norm_shift, qkv_weight, qkv_bias, up_weight, up_bias, out_weight, out_bias, down_weight, down_bias, grad_output):
    qkv_flat = qkv_weight.reshape(D, 3 * D)
    bias_flat = qkv_bias.reshape(3 * D)
    cosine, sine_table = rotary_tables(SEQ_LEN)
    inputs = layer_input.reshape(-1, SEQ_LEN, D)
    cotangents = grad_output.reshape(-1, SEQ_LEN, D)

    def one_sequence(carry, pair):
        block, grad_block = pair
        xfloat = block.astype(jnp.float32)
        mean_val = lax.optimization_barrier(jnp.mean(xfloat, axis=1, keepdims=True))
        spread = lax.optimization_barrier(jnp.mean(xfloat * xfloat, axis=1, keepdims=True)) - mean_val * mean_val
        inv_std = lax.rsqrt(spread + eps_norm)
        normed = (xfloat - mean_val) * inv_std
        hidden_in = (normed * norm_gain + norm_shift).astype(jnp.bfloat16)
        projected = jnp.dot(hidden_in, qkv_flat, preferred_element_type=jnp.float32) + bias_flat
        upper = jnp.dot(hidden_in, up_weight, preferred_element_type=jnp.float32) + up_bias
        parts = projected.reshape(SEQ_LEN, 3, HEADS, HEAD)
        query = rotate(parts[:, 0], cosine, sine_table).astype(jnp.bfloat16)
        keys = rotate(parts[:, 1], cosine, sine_table).astype(jnp.bfloat16)
        values = parts[:, 2].astype(jnp.bfloat16)
        attended, log_total = attend(query, keys, values)
        mixed = attended.reshape(SEQ_LEN, D)
        activated = gelu_tanh(upper).astype(jnp.bfloat16)
        result = xfloat + jnp.dot(mixed, out_weight, preferred_element_type=jnp.float32) + out_bias
        result = result + jnp.dot(activated, down_weight, preferred_element_type=jnp.float32) + down_bias
        out_block = result.astype(jnp.bfloat16)
        grad_float = grad_block.astype(jnp.float32)
        bias_out_step = lax.optimization_barrier(jnp.sum(grad_float, axis=0))
        out_w_step = jnp.dot(mixed.T, grad_block, preferred_element_type=jnp.float32)
        down_w_step = jnp.dot(activated.T, grad_block, preferred_element_type=jnp.float32)
        grad_mixed = jnp.dot(grad_block, out_weight.T, preferred_element_type=jnp.float32).astype(jnp.bfloat16)
        grad_act = jnp.dot(grad_block, down_weight.T, preferred_element_type=jnp.float32)
        grad_upper = (grad_act * gelu_slope(upper)).astype(jnp.bfloat16)
        grad_query, grad_keys, grad_values = attend_back(query, keys, values, attended, grad_mixed.reshape(SEQ_LEN, HEADS, HEAD), log_total)
        grad_query = unrotate(grad_query, cosine, sine_table)
        grad_keys = unrotate(grad_keys, cosine, sine_table)
        grad_proj = jnp.stack([grad_query, grad_keys, grad_values], axis=1).reshape(SEQ_LEN, 3 * D).astype(jnp.bfloat16)
        qkv_b_step = lax.optimization_barrier(jnp.sum(grad_proj.astype(jnp.float32), axis=0))
        up_b_step = lax.optimization_barrier(jnp.sum(grad_upper.astype(jnp.float32), axis=0))
        qkv_w_step = jnp.dot(hidden_in.T, grad_proj, preferred_element_type=jnp.float32)
        up_w_step = jnp.dot(hidden_in.T, grad_upper, preferred_element_type=jnp.float32)
        grad_hidden = jnp.dot(grad_proj, qkv_flat.T, preferred_element_type=jnp.float32)
        grad_hidden = grad_hidden + jnp.dot(grad_upper, up_weight.T, preferred_element_type=jnp.float32)
        gain_step = lax.optimization_barrier(jnp.sum(grad_hidden * normed, axis=0))
        shift_step = lax.optimization_barrier(jnp.sum(grad_hidden, axis=0))
        grad_normed = grad_hidden * norm_gain
        first_mean = lax.optimization_barrier(jnp.mean(grad_normed, axis=1, keepdims=True))
        second_mean = lax.optimization_barrier(jnp.mean(grad_normed * normed, axis=1, keepdims=True))
        grad_in = grad_float + inv_std * (grad_normed - first_mean - normed * second_mean)
        steps_now = (gain_step, shift_step, qkv_w_step, qkv_b_step, up_w_step, up_b_step, out_w_step, bias_out_step, down_w_step)
        carry = tuple((old + new for old, new in zip(carry, steps_now)))
        return (carry, (out_block, grad_in))
    start = (jnp.zeros((D,), jnp.float32), jnp.zeros((D,), jnp.float32), jnp.zeros((D, 3 * D), jnp.float32), jnp.zeros((3 * D,), jnp.float32), jnp.zeros((D, FF), jnp.float32), jnp.zeros((FF,), jnp.float32), jnp.zeros((D, D), jnp.float32), jnp.zeros((D,), jnp.float32), jnp.zeros((FF, D), jnp.float32))
    sums, stacked = lax.scan(one_sequence, start, (inputs, cotangents))
    layer_output = stacked[0].reshape(-1, D)
    grad_input = stacked[1].reshape(-1, D)
    grad_gain, grad_shift, grad_qkv_w, grad_qkv_b, grad_up_w, grad_up_b, grad_out_w, grad_bias_out, grad_down_w = sums
    return (layer_output, grad_input, grad_gain, grad_shift, grad_qkv_w.reshape(D, 3, D), grad_qkv_b.reshape(3, D), grad_up_w, grad_up_b, grad_out_w, grad_bias_out, grad_down_w, grad_bias_out)
```

```python
import functools
import math

import jax
import jax.numpy as jnp
from jax import lax
from jax.experimental import pallas as pl
from jax.experimental.pallas import tpu as pltpu
from jax.sharding import Mesh, PartitionSpec as P


HEAD = 64
ROT = 32
SEQ_LEN = 1024
BLOCK = 256

eps_norm = 1e-05
gelu_scale = 0.7978845608028654
gelu_cubic = 0.044715

SWAP = [(0, 1), (1, 0)]
TURN = [(0, 0), (1, 2), (2, 3), (3, 1)]
UNTURN = [(b, a) for a, b in TURN]


def gelu_tanh(value):
    inner = gelu_scale * (value + gelu_cubic * value * value * value)
    return 0.5 * value * (1.0 + jnp.tanh(inner))


def gelu_slope(value):
    inner = gelu_scale * (value + gelu_cubic * value * value * value)
    tanh_val = jnp.tanh(inner)
    return 0.5 * (1.0 + tanh_val) + 0.5 * value * (1.0 - tanh_val * tanh_val) * gelu_scale * (
        1.0 + 3.0 * gelu_cubic * value * value
    )


def rotary_tables(length, heads):
    positions = jnp.arange(length).astype(jnp.float32)
    frequency = jnp.exp(-math.log(10000.0) * jnp.arange(0, ROT, 2).astype(jnp.float32) / ROT)
    angles = positions[:, None] * frequency[None, :]
    cosine, sine = jnp.cos(angles), jnp.sin(angles)
    zero = jnp.zeros_like(sine)
    rest = HEAD - ROT
    keep = jnp.concatenate([cosine, cosine, jnp.ones((length, rest), jnp.float32)], axis=1)
    ahead = jnp.concatenate([-sine, zero, jnp.zeros((length, rest), jnp.float32)], axis=1)
    behind = jnp.concatenate([zero, sine, jnp.zeros((length, rest), jnp.float32)], axis=1)
    return tuple(jnp.tile(t, (1, heads)) for t in (keep, ahead, behind))


def lanes_of(shape, head):
    place = lax.broadcasted_iota(jnp.int32, shape, 1)
    return (place >= head * HEAD) & (place < (head + 1) * HEAD)


def attend_forward_kernel(proj, bias, keep, ahead, behind, query, keys, values, out, log_total, value_t, out_t):
    length, width = out.shape
    heads = width // HEAD
    half = ROT // 2

    def turned(field):
        return (
            field * keep[...]
            + pltpu.roll(field, width - half, 1) * ahead[...]
            + pltpu.roll(field, half, 1) * behind[...]
        )

    query[...] = turned(proj[:, :width] + bias[:, :width]).astype(jnp.bfloat16)
    keys[...] = turned(proj[:, width : 2 * width] + bias[:, width : 2 * width]).astype(jnp.bfloat16)
    val = proj[:, 2 * width :] + bias[:, 2 * width :]
    values[...] = val.astype(jnp.bfloat16)
    value_t[...] = val.T.astype(jnp.bfloat16)

    def one_head(head, carry):
        start = pl.multiple_of(head * HEAD, HEAD)
        for begin in range(0, length, BLOCK):
            end = begin + BLOCK
            block = query[begin:end, :]
            block = jnp.where(lanes_of(block.shape, head), block * jnp.bfloat16(HEAD**-0.5), jnp.bfloat16(0))
            scores = lax.dot_general(
                keys[:end, :], block, (((1,), (1,)), ((), ())), preferred_element_type=jnp.float32
            )
            place = lax.broadcasted_iota(jnp.int32, (BLOCK, BLOCK), 0)
            asker = lax.broadcasted_iota(jnp.int32, (BLOCK, BLOCK), 1)
            last = jnp.where(place <= asker, scores[begin:end], -1e30)
            scores = last if begin == 0 else jnp.concatenate([scores[:begin], last], axis=0)
            peak = jnp.max(scores, axis=0, keepdims=True)
            raised = jnp.exp(scores - peak)
            total = jnp.sum(raised, axis=0, keepdims=True)
            weights = (raised * (1.0 / total)).astype(jnp.bfloat16)
            log_total[0, pl.ds(head, 1), begin:end] = peak + jnp.log(total)
            out_t[pl.ds(start, HEAD), begin:end] = jnp.dot(
                value_t[pl.ds(start, HEAD), :end], weights, preferred_element_type=jnp.float32
            )
        return carry

    lax.fori_loop(0, heads, one_head, 0)
    out[...] = out_t[...].T.astype(jnp.bfloat16)


def attend_forward(proj, bias, tables):
    tokens, width3 = proj.shape
    width = width3 // 3
    sequences = tokens // SEQ_LEN
    heads = width // HEAD
    rows = pl.BlockSpec((SEQ_LEN, width), lambda s: (s, 0))
    table = pl.BlockSpec((SEQ_LEN, width), lambda s: (0, 0))
    flops = 4 * tokens * SEQ_LEN * width
    return pl.pallas_call(
        attend_forward_kernel,
        grid=(sequences,),
        in_specs=[
            pl.BlockSpec((SEQ_LEN, width3), lambda s: (s, 0)),
            pl.BlockSpec((1, width3), lambda s: (0, 0)),
            table,
            table,
            table,
        ],
        out_specs=[rows, rows, rows, rows, pl.BlockSpec((1, heads, SEQ_LEN), lambda s: (s, 0, 0))],
        out_shape=[jax.ShapeDtypeStruct((tokens, width), jnp.bfloat16)] * 4
        + [jax.ShapeDtypeStruct((sequences, heads, SEQ_LEN), jnp.float32)],
        scratch_shapes=[pltpu.VMEM((width, SEQ_LEN), jnp.bfloat16), pltpu.VMEM((width, SEQ_LEN), jnp.float32)],
        cost_estimate=pl.CostEstimate(
            flops=4 * flops, bytes_accessed=tokens * width * 20, transcendentals=tokens * SEQ_LEN * heads // 2
        ),
        name="attend_forward",
    )(proj, bias, *tables)


def attend_backward_kernel(
    query, keys, values, out, grad_out, log_total, keep, ahead, behind, *rest
):
    grad, key_t, product_t, grad_q, grad_k, grad_v = rest[-6:]
    length, width = out.shape
    heads = width // HEAD
    half = ROT // 2
    scale = jnp.bfloat16(HEAD**-0.5)
    key_t[...] = (keys[...].astype(jnp.float32) * HEAD**-0.5).T.astype(jnp.bfloat16)
    product_t[...] = (grad_out[...].astype(jnp.float32) * out[...].astype(jnp.float32)).T
    grad_k[...] = jnp.zeros_like(grad_k)
    grad_v[...] = jnp.zeros_like(grad_v)

    def one_head(head, carry):
        start = pl.multiple_of(head * HEAD, HEAD)
        for begin in range(0, length, BLOCK):
            end = begin + BLOCK
            mine = lanes_of((BLOCK, width), head)
            block = jnp.where(mine, query[begin:end, :] * scale, jnp.bfloat16(0))
            grad_block = jnp.where(mine, grad_out[begin:end, :], jnp.bfloat16(0))
            dims = (((1,), (1,)), ((), ()))
            scores = lax.dot_general(keys[:end, :], block, dims, preferred_element_type=jnp.float32)
            along = lax.dot_general(values[:end, :], grad_block, dims, preferred_element_type=jnp.float32)
            delta = jnp.sum(product_t[pl.ds(start, HEAD), begin:end], axis=0, keepdims=True)
            place = lax.broadcasted_iota(jnp.int32, (BLOCK, BLOCK), 0)
            asker = lax.broadcasted_iota(jnp.int32, (BLOCK, BLOCK), 1)
            last = jnp.where(place <= asker, scores[begin:end], -1e30)
            scores = last if begin == 0 else jnp.concatenate([scores[:begin], last], axis=0)
            probs = jnp.exp(scores - log_total[0, pl.ds(head, 1), begin:end])
            grad_scores = (probs * (along - delta)).astype(jnp.bfloat16)
            grad_v[:end, :] += jnp.dot(probs.astype(jnp.bfloat16), grad_block, preferred_element_type=jnp.float32)
            grad_k[:end, :] += jnp.dot(grad_scores, block, preferred_element_type=jnp.float32)
            grad_q[pl.ds(start, HEAD), begin:end] = jnp.dot(
                key_t[pl.ds(start, HEAD), :end], grad_scores, preferred_element_type=jnp.float32
            )
        return carry

    lax.fori_loop(0, heads, one_head, 0)

    def back(field):
        return (
            field * keep[...]
            - pltpu.roll(field, width - half, 1) * ahead[...]
            - pltpu.roll(field, half, 1) * behind[...]
        ).astype(jnp.bfloat16)

    grad[:, :width] = back(grad_q[...].T)
    grad[:, width : 2 * width] = back(grad_k[...])
    grad[:, 2 * width :] = grad_v[...].astype(jnp.bfloat16)


def attend_backward(query, keys, values, out, grad_out, log_total, tables, sequence, filled=None):
    tokens, width = query.shape
    heads = width // HEAD
    rows = pl.BlockSpec((SEQ_LEN, width), lambda s: (sequence, 0))
    table = pl.BlockSpec((SEQ_LEN, width), lambda s: (0, 0))
    flops = 4 * SEQ_LEN * SEQ_LEN * width
    extras = [] if filled is None else [filled]
    return pl.pallas_call(
        attend_backward_kernel,
        grid=(1,),
        in_specs=[rows] * 5
        + [pl.BlockSpec((1, heads, SEQ_LEN), lambda s: (sequence, 0, 0))]
        + [table] * 3
        + [pl.BlockSpec(memory_space=pl.ANY) for _ in extras],
        out_specs=pl.BlockSpec((SEQ_LEN, 3 * width), lambda s: (sequence, 0)),
        out_shape=jax.ShapeDtypeStruct((tokens, 3 * width), jnp.bfloat16),
        scratch_shapes=[
            pltpu.VMEM((width, SEQ_LEN), jnp.bfloat16),
            pltpu.VMEM((width, SEQ_LEN), jnp.float32),
            pltpu.VMEM((width, SEQ_LEN), jnp.float32),
            pltpu.VMEM((SEQ_LEN, width), jnp.float32),
            pltpu.VMEM((SEQ_LEN, width), jnp.float32),
        ],
        input_output_aliases={9: 0} if extras else {},
        cost_estimate=pl.CostEstimate(
            flops=8 * flops, bytes_accessed=SEQ_LEN * width * 24, transcendentals=SEQ_LEN * SEQ_LEN * heads // 2
        ),
        name="attend_backward",
    )(query, keys, values, out, grad_out, log_total, *tables, *extras)


def normalize_kernel(x, gain, shift, own, other, hidden, stats, projected):
    half = x.shape[2]
    left, right = x[0].astype(jnp.float32), x[1].astype(jnp.float32)
    width = 2 * half
    mean = (jnp.sum(left, axis=1, keepdims=True) + jnp.sum(right, axis=1, keepdims=True)) / width
    square = jnp.sum(left * left, axis=1, keepdims=True) + jnp.sum(right * right, axis=1, keepdims=True)
    inv_std = lax.rsqrt(square / width - mean * mean + eps_norm)
    left = ((left - mean) * inv_std * gain[0] + shift[0]).astype(jnp.bfloat16)
    right = ((right - mean) * inv_std * gain[1] + shift[1]).astype(jnp.bfloat16)
    hidden[:, :half] = left
    hidden[:, half:] = right
    stats[:, :1] = mean
    stats[:, 1:] = inv_std
    projected[...] = jnp.dot(left, own[...], preferred_element_type=jnp.float32) + jnp.dot(
        right, other[...], preferred_element_type=jnp.float32
    )


def normalize_project(x_line, gain, shift, own, other):
    _, tokens, half = x_line.shape
    columns = own.shape[1]
    rows = 256
    vector = pl.BlockSpec((2, 1, half), lambda i: (0, 0, 0))
    weight = pl.BlockSpec((half, columns), lambda i: (0, 0))

    def tall(width):
        return pl.BlockSpec((rows, width), lambda i: (i, 0))

    return pl.pallas_call(
        normalize_kernel,
        grid=(tokens // rows,),
        in_specs=[pl.BlockSpec((2, rows, half), lambda i: (0, i, 0)), vector, vector, weight, weight],
        out_specs=[tall(2 * half), tall(2), tall(columns)],
        out_shape=[
            jax.ShapeDtypeStruct((tokens, 2 * half), jnp.bfloat16),
            jax.ShapeDtypeStruct((tokens, 2), jnp.float32),
            jax.ShapeDtypeStruct((tokens, columns), jnp.float32),
        ],
        cost_estimate=pl.CostEstimate(
            flops=4 * tokens * half * columns, bytes_accessed=tokens * half * 14, transcendentals=tokens
        ),
        name="normalize_project",
    )(x_line, gain, shift, own, other)


def raise_kernel(hidden, own, other, bias, activated, upper):
    half = own.shape[0]
    value = jnp.dot(hidden[:, :half], own[...], preferred_element_type=jnp.float32)
    value += jnp.dot(hidden[:, half:], other[...], preferred_element_type=jnp.float32)
    value += bias[...]
    upper[...] = value
    activated[...] = gelu_tanh(value).astype(jnp.bfloat16)


def raise_units(hidden, own, other, bias):
    tokens, width = hidden.shape
    half, columns = own.shape
    rows = 256
    weight = pl.BlockSpec((half, columns), lambda i: (0, 0))
    out = pl.BlockSpec((rows, columns), lambda i: (i, 0))
    return pl.pallas_call(
        raise_kernel,
        grid=(tokens // rows,),
        in_specs=[
            pl.BlockSpec((rows, width), lambda i: (i, 0)),
            weight,
            weight,
            pl.BlockSpec((1, columns), lambda i: (0, 0)),
        ],
        out_specs=[out, out],
        out_shape=[
            jax.ShapeDtypeStruct((tokens, columns), jnp.bfloat16),
            jax.ShapeDtypeStruct((tokens, columns), jnp.float32),
        ],
        cost_estimate=pl.CostEstimate(
            flops=2 * tokens * width * columns, bytes_accessed=tokens * columns * 12, transcendentals=tokens * columns
        ),
        name="raise_units",
    )(hidden, own, other, bias)


NT = (((1,), (1,)), ((), ()))


def fetch(place, own, other, into, semaphore):
    @pl.when(pl.program_id(0) == 0)
    def _():
        for index, block in enumerate((own, other)):

            @pl.when(place[0] == index)
            def _(block=block):
                copy = pltpu.make_async_copy(block, into, semaphore)
                copy.start()
                copy.wait()


def two_products_kernel(first, place, left, right, own, other, *rest):
    *extra, out, weight, semaphore = rest
    fetch(place, own, other, weight, semaphore)
    total = jnp.dot(left[...], weight[:first], preferred_element_type=jnp.float32)
    total += jnp.dot(right[...], weight[first:], preferred_element_type=jnp.float32)
    if extra:
        total += extra[0][...].astype(jnp.float32)
    out[...] = total.astype(jnp.bfloat16)


def two_products(place, left, right, own, other, extra=None):
    tokens, first = left.shape
    second, half = right.shape[1], own.shape[1]
    rows = min(512, tokens)

    def tall(columns):
        return pl.BlockSpec((rows, columns), lambda i, s: (i, 0))

    anywhere = pl.BlockSpec(memory_space=pl.ANY)
    extras = [] if extra is None else [extra]
    return pl.pallas_call(
        functools.partial(two_products_kernel, first),
        grid_spec=pltpu.PrefetchScalarGridSpec(
            num_scalar_prefetch=1,
            grid=(tokens // rows,),
            in_specs=[tall(first), tall(second), anywhere, anywhere, *(tall(half) for _ in extras)],
            out_specs=tall(half),
            scratch_shapes=[pltpu.VMEM(own.shape, own.dtype), pltpu.SemaphoreType.DMA],
        ),
        out_shape=jax.ShapeDtypeStruct((tokens, half), jnp.bfloat16),
        cost_estimate=pl.CostEstimate(
            flops=2 * tokens * (first + second) * half,
            bytes_accessed=2 * (tokens * (first + second + half) + (first + second) * half),
            transcendentals=0,
        ),
        name="two_products",
    )(place, left, right, own, other, *extras)


def two_products_t_kernel(place, left, right, left_own, left_other, right_own, right_other, *rest):
    *extra, out, left_w, right_w, semaphores = rest
    fetch(place, left_own, left_other, left_w, semaphores.at[0])
    fetch(place, right_own, right_other, right_w, semaphores.at[1])
    total = lax.dot_general(left[...], left_w[...], NT, preferred_element_type=jnp.float32)
    total += lax.dot_general(right[...], right_w[...], NT, preferred_element_type=jnp.float32)
    if extra:
        total += extra[0][...].astype(jnp.float32)
    out[...] = total.astype(jnp.bfloat16)


def two_products_t(place, left, right, left_w, right_w, extra=None):
    tokens, first = left.shape
    second, half = right.shape[1], left_w[0].shape[0]
    rows = min(512, tokens)

    def tall(columns):
        return pl.BlockSpec((rows, columns), lambda i, s: (i, 0))

    anywhere = pl.BlockSpec(memory_space=pl.ANY)
    extras = [] if extra is None else [extra]
    return pl.pallas_call(
        two_products_t_kernel,
        grid_spec=pltpu.PrefetchScalarGridSpec(
            num_scalar_prefetch=1,
            grid=(tokens // rows,),
            in_specs=[tall(first), tall(second)] + [anywhere] * 4 + [tall(half) for _ in extras],
            out_specs=tall(half),
            scratch_shapes=[
                pltpu.VMEM((half, first), jnp.bfloat16),
                pltpu.VMEM((half, second), jnp.bfloat16),
                pltpu.SemaphoreType.DMA((2,)),
            ],
        ),
        out_shape=jax.ShapeDtypeStruct((tokens, half), jnp.bfloat16),
        cost_estimate=pl.CostEstimate(
            flops=2 * tokens * (first + second) * half,
            bytes_accessed=2 * (tokens * (first + second + half) + (first + second) * half),
            transcendentals=0,
        ),
        name="two_products_t",
    )(place, left, right, *left_w, *right_w, *extras)


def into_units_kernel(grad, own, other, slope, mixed, upper, bias):
    attn = mixed.shape[1]

    @pl.when(pl.program_id(0) == 0)
    def _():
        bias[...] = jnp.zeros_like(bias)

    def back(low, high):
        total = lax.dot_general(grad[0], own[low:high], NT, preferred_element_type=jnp.float32)
        return total + lax.dot_general(grad[1], other[low:high], NT, preferred_element_type=jnp.float32)

    mixed[...] = back(0, attn).astype(jnp.bfloat16)
    value = (back(attn, own.shape[0]) * slope[...]).astype(jnp.bfloat16)
    upper[...] = value
    bias[...] += jnp.sum(value.astype(jnp.float32), axis=0, keepdims=True)


def into_units(grad, own, other, slope, attn):
    _, tokens, half = grad.shape
    units = own.shape[0]
    rows = min(256, tokens)
    weight = pl.BlockSpec((units, half), lambda i: (0, 0))
    return pl.pallas_call(
        into_units_kernel,
        grid=(tokens // rows,),
        in_specs=[
            pl.BlockSpec((2, rows, half), lambda i: (0, i, 0)),
            weight,
            weight,
            pl.BlockSpec((rows, units - attn), lambda i: (i, 0)),
        ],
        out_specs=[
            pl.BlockSpec((rows, attn), lambda i: (i, 0)),
            pl.BlockSpec((rows, units - attn), lambda i: (i, 0)),
            pl.BlockSpec((1, units - attn), lambda i: (0, 0)),
        ],
        out_shape=[
            jax.ShapeDtypeStruct((tokens, attn), jnp.bfloat16),
            jax.ShapeDtypeStruct((tokens, units - attn), jnp.bfloat16),
            jax.ShapeDtypeStruct((1, units - attn), jnp.float32),
        ],
        cost_estimate=pl.CostEstimate(
            flops=4 * tokens * units * half, bytes_accessed=8 * tokens * half, transcendentals=0
        ),
        name="into_units",
    )(grad, own, other, slope)


def contract_rows(left, right):
    return lax.dot_general(left, right, (((0,), (0,)), ((), ())), preferred_element_type=jnp.float32)


def after(value, *earlier):
    return lax.optimization_barrier((value, *earlier))[0]


def sum_over(value, axes):
    for axis in axes:
        size = lax.axis_size(axis)
        if size & (size - 1):
            value = lax.psum(value, axis)
            continue
        step = 1
        while step < size:
            value = value + lax.ppermute(value, axis, [(i, i ^ step) for i in range(size)])
            step *= 2
    return value


def in_order(place, own, other, axis):
    return jnp.where(
        place == 0, jnp.concatenate([own, other], axis=axis), jnp.concatenate([other, own], axis=axis)
    )


def shards(
    layer_input,
    norm_gain,
    norm_shift,
    qkv_weight,
    qkv_bias,
    up_weight,
    up_bias,
    out_weight,
    out_bias,
    down_weight,
    down_bias,
    grad_output,
):
    bf16, f32 = jnp.bfloat16, jnp.float32
    pod, core, row, col = (lax.axis_index(name) for name in ("pod", "core", "row", "col"))
    pods, cols = lax.axis_size("pod"), lax.axis_size("col")
    quarter, half = layer_input.shape
    width = 2 * half
    line_tokens = quarter * cols
    attn = qkv_weight.shape[2] // 2
    ff = up_weight.shape[1] // 2

    def move(value, axis, pairs, *earlier):
        return lax.ppermute(after(value, *earlier) if earlier else value, axis, pairs)

    qkv_own = lax.dynamic_slice_in_dim(qkv_weight, core * attn, attn, 2).reshape(half, 3 * attn)
    up_own = lax.dynamic_slice_in_dim(up_weight, core * ff, ff, 1)
    out_own = lax.dynamic_slice_in_dim(out_weight, core * attn, attn, 0)
    down_own = lax.dynamic_slice_in_dim(down_weight, core * ff, ff, 0)
    mix_own = jnp.concatenate([out_own, down_own], axis=0)
    small = jnp.stack([norm_gain, norm_shift])

    def part_of(value):
        if pods % 2:
            return value
        size = value.shape[0] // 2
        return lax.dynamic_slice_in_dim(value, (pod % 2) * size, size, 0)

    def both_parts(part, *earlier):
        if pods % 2:
            return part
        part = after(part, *earlier) if earlier else part
        other = move(part, "pod", [(i, i ^ 1) for i in range(pods)])
        return part, other

    def joined(parts, *earlier):
        if pods % 2:
            return parts
        mine, other = after(parts, *earlier) if earlier else parts
        return in_order(pod % 2, mine, other, 0)

    x_turned = move(layer_input, ("core", "row"), TURN)
    x_line = lax.all_gather(x_turned, ("core", "col"), axis=0, tiled=True).reshape(2, line_tokens, half)
    qkv_other = move(qkv_own, "row", SWAP, x_turned)
    small_other = move(small, "row", SWAP, x_turned)
    g_turned = move(grad_output, ("core", "row"), TURN, qkv_other)
    g_line = lax.all_gather(g_turned, ("core", "col"), axis=0, tiled=True).reshape(2, line_tokens, half)
    up_part = move(part_of(up_own), "row", SWAP, g_turned)
    up_parts = both_parts(up_part)
    mix_part = move(part_of(mix_own), "row", SWAP, up_part)

    gain, shift = jnp.concatenate([small, small_other], axis=1)
    bias_qkv = lax.dynamic_slice_in_dim(qkv_bias, core * attn, attn, 1).reshape(1, 3 * attn)
    bias_up = lax.dynamic_slice_in_dim(up_bias, core * ff, ff, 0).reshape(1, ff)
    tables = rotary_tables(SEQ_LEN, attn // HEAD)
    keep_at, send_at = core.reshape(1), (1 - core).reshape(1)

    x_line = after(x_line, gain, *tables)
    hidden, stats_line, projected = normalize_project(
        x_line, gain.reshape(2, 1, half), shift.reshape(2, 1, half), qkv_own, qkv_other
    )
    mix_parts = both_parts(mix_part, stats_line)
    query, keys, values, mixed, log_total = attend_forward(projected, bias_qkv, tables)
    up_other = joined(up_parts, stats_line)
    activated, upper = raise_units(hidden, up_own, up_other, after(bias_up, mixed))
    mix_other = joined(mix_parts, mixed)
    result_send = two_products(send_at, mixed, activated, mix_own, mix_other)
    result_recv = move(result_send, "core", SWAP)
    slope = gelu_slope(after(upper, result_send))
    result = two_products(keep_at, mixed, activated, mix_own, mix_other, result_recv)
    result_mine = lax.psum_scatter(result, "col", scatter_dimension=0, tiled=True)

    def product(left, right):
        return contract_rows(left, right).astype(bf16)

    def pod_sum(left, right, received):
        total = (contract_rows(left, right) + received.astype(f32)).astype(bf16)
        if pods == 2:
            return total, lax.ppermute(total, "pod", SWAP)
        return lax.psum(total, "pod"), None

    def core_swap(total, received):
        if received is not None:
            total = (total.astype(f32) + received.astype(f32)).astype(bf16)
        return total, move(total, "core", SWAP)

    g_line = after(g_line, result, slope)
    g_keep, g_send = g_line[0], g_line[1]
    h_keep, h_send = hidden[:, :half], hidden[:, half:]
    act_a, act_b = activated[:, : ff // 2], activated[:, ff // 2 :]
    out_send = product(mixed, g_send)
    out_recv = move(out_send, "row", SWAP)
    da_send = product(act_a, after(g_send, out_send))
    da_recv = move(da_send, "row", SWAP)
    grad_mixed, grad_upper, up_b = into_units(after(g_line, da_send), mix_own, mix_other, slope, attn)
    out_pod = pod_sum(mixed, after(g_keep, grad_upper), out_recv)
    db_send = product(act_b, after(g_send, out_pod[0]))
    db_recv = move(db_send, "row", SWAP, out_recv)
    grad_proj = attend_backward(query, keys, values, mixed, after(grad_mixed, db_send), log_total, tables, 0)
    da_pod = pod_sum(act_a, after(g_keep, grad_proj), da_recv)
    for index in range(1, line_tokens // SEQ_LEN):
        grad_proj = attend_backward(
            query, keys, values, mixed, after(grad_mixed, da_pod[0]), log_total, tables, index, grad_proj
        )
    up_send = product(h_send, after(grad_upper, grad_proj))
    up_recv = move(up_send, "row", SWAP)
    into = after(grad_proj, up_send, result_mine)
    qkv_w, up_w = (qkv_own, qkv_other), (up_own, up_other)
    hid_send = two_products_t(send_at, into, grad_upper, qkv_w, up_w)
    hid_recv = move(hid_send, "core", SWAP)
    db_pod = pod_sum(act_b, after(g_keep, hid_send), db_recv)
    grad_hidden = two_products_t(keep_at, after(into, db_pod[0]), grad_upper, qkv_w, up_w, hid_recv)
    grad_mine = lax.psum_scatter(grad_hidden, "col", scatter_dimension=0, tiled=True)
    qkv_send = product(h_send, after(grad_proj, grad_hidden))
    qkv_recv = move(qkv_send, "row", SWAP, up_recv)

    grad_float = grad_hidden.astype(f32)
    x_keep = lax.dynamic_index_in_dim(x_line, core, 0, keepdims=False).astype(f32)
    normed_keep = (x_keep - stats_line[:, :1]) * stats_line[:, 1:]
    zeros = functools.partial(jnp.zeros, dtype=f32)

    def slot(value, places, place):
        wide = zeros((places,) + value.shape)
        return lax.dynamic_update_index_in_dim(wide, value, place, 0)

    part = core + 2 * col
    pieces = [
        slot(jnp.sum(grad_float * normed_keep, axis=0), 2, core ^ row),
        slot(jnp.sum(grad_float, axis=0), 2, core ^ row),
        slot(jnp.sum(grad_output.astype(f32), axis=0), 2, row),
        slot(jnp.sum(grad_proj.astype(f32), axis=0), 2 * cols, part),
        slot(up_b.reshape(ff), 2 * cols, part),
    ]
    sums = sum_over(jnp.concatenate([p.reshape(-1) for p in pieces]), ("core", "row", "pod", "col"))
    up_pod = pod_sum(h_keep, after(grad_upper, sums), up_recv)
    qkv_pod = pod_sum(h_keep, after(grad_proj, up_pod[0]), qkv_recv)
    taken = []
    at = 0
    for piece in pieces:
        taken.append(sums[at : at + piece.size].reshape(piece.shape))
        at += piece.size
    grad_gain = lax.dynamic_index_in_dim(taken[0], row, 0, keepdims=False)
    grad_shift = lax.dynamic_index_in_dim(taken[1], row, 0, keepdims=False)
    grad_bias_out = lax.dynamic_index_in_dim(taken[2], row, 0, keepdims=False)
    qkv_b = lax.dynamic_slice_in_dim(taken[3], 2 * col, 2, 0).reshape(2, 3, attn)
    grad_qkv_b = jnp.concatenate([qkv_b[0], qkv_b[1]], axis=1)
    grad_up_b = lax.dynamic_slice_in_dim(taken[4], 2 * col, 2, 0).reshape(2 * ff)

    result_home = move(result_mine, ("core", "row"), UNTURN, sums)
    layer_output = (
        layer_input.astype(f32) + result_home.astype(f32) + out_bias + down_bias
    ).astype(bf16)
    x_home = layer_input.astype(f32)
    stats = jnp.stack([jnp.sum(x_home, axis=1), jnp.sum(x_home * x_home, axis=1)])
    stats = stats + move(stats, "row", SWAP, sums)
    mean_home = stats[0] / width
    inv_home = lax.rsqrt(stats[1] / width - mean_home * mean_home + eps_norm)
    normed_home = (x_home - mean_home[:, None]) * inv_home[:, None]
    grad_back = move(grad_mine, ("core", "row"), UNTURN, inv_home).astype(f32)
    grad_normed = grad_back * norm_gain
    totals = jnp.stack([jnp.sum(grad_normed, axis=1), jnp.sum(grad_normed * normed_home, axis=1)])
    totals = totals + move(totals, "row", SWAP)
    grad_input = grad_output.astype(f32) + inv_home[:, None] * (
        grad_normed - totals[0][:, None] / width - normed_home * totals[1][:, None] / width
    )

    out_a, out_b = core_swap(*out_pod)
    da_a, da_b = core_swap(*da_pod)
    db_a, db_b = core_swap(*db_pod)
    up_a, up_b2 = core_swap(*up_pod)
    qkv_a, qkv_b2 = core_swap(*qkv_pod)
    grad_out_w = in_order(core, out_a, out_b, 0).astype(f32)
    down_a = jnp.concatenate([da_a, db_a], axis=0)
    down_b = jnp.concatenate([da_b, db_b], axis=0)
    grad_down_w = in_order(core, down_a, down_b, 0).astype(f32)
    grad_up_w = in_order(core, up_a, up_b2, 1).astype(f32)
    grad_qkv_w = in_order(
        core, qkv_a.reshape(half, 3, attn), qkv_b2.reshape(half, 3, attn), 2
    ).astype(f32)
    return (
        layer_output,
        grad_input,
        grad_gain,
        grad_shift,
        grad_qkv_w,
        grad_qkv_b,
        grad_up_w,
        grad_up_b,
        grad_out_w,
        grad_bias_out,
        grad_down_w,
        grad_bias_out,
    )


def solution(mesh):
    groups, rows, cols = (mesh.shape[name] for name in ("dp", "row", "col"))
    fine = Mesh(mesh.devices.reshape(groups // 2, 2, rows, cols), ("pod", "core", "row", "col"))
    tokens = P(("pod", "core", "col"), "row")
    specs = (
        P("row"),
        P("row"),
        P("row", None, "col"),
        P(None, "col"),
        P("row", "col"),
        P("col"),
        P("col", "row"),
        P("row"),
        P("col", "row"),
        P("row"),
    )

    return jax.shard_map(
        shards,
        mesh=fine,
        in_specs=(tokens, *specs, tokens),
        out_specs=(tokens, tokens, *specs),
        check_vma=False,
    )
```
